256 devices in a mesh: req: 64 (over x, y, z_hi), tp: 4 (over z_lo, core).
Axes of the slice: x: 4, y: 4, z: 8 (z_hi: 4, z_lo: 2; z = z_hi * 2 + z_lo), core: 2. Of those that a mesh axis runs over, the one named last changes fastest.
Arguments:
- hidden: bfloat16 [64, 256, 4, 2432], P('req'), may hold values from -4 to 4
- modulation: bfloat16 [16, 4, 3, 2432], replicated, may hold values from -4 to 4
- w_qkv: bfloat16 [2432, 3, 1536], P(None, None, 'tp'), may hold values from -0.125 to 0.125
- w_out: bfloat16 [1536, 2432], P('tp'), may hold values from -0.75 to 0.75
- qk_gain: float32 [2, 64], replicated, may hold values from 0.1 to 1.9
- stale_kv: bfloat16 [64, 256, 4, 2, 1536], P('req', None, None, None, 'tp'), may hold values from -5 to 5
- text_kv: bfloat16 [64, 40, 4, 2, 1536], P('req', None, None, None, 'tp'), may hold values from -5 to 5
- text_len: int32 [16, 4], replicated, may hold values from 1 to 160, as said below
Outputs:
- updated: bfloat16 [64, 256, 4, 2432], P('req', 'tp')
- fresh_kv: bfloat16 [64, 256, 4, 2, 1536], P('req', None, None, None, 'tp')
The draws below stay inside these ranges and needn't reach their ends.
Inputs may be any that keep to these rules, and one draw needn't show every extreme that they name: `text_len`: some item has all 160 text tokens valid in every draw.
All inputs are finite; a program needn't handle non-finite values.
Results may differ from the reference program's by a relative error of at most 0.015.
Values may be sent and summed in bfloat16 or wider, within the bound.
No kernel may reach another device: no remote copies, remote signals or barrier semaphores. Data moves between devices by JAX's collectives and lax.ppermute only.
A program may use at most 128 MiB of HBM per device.

```python
import jax
import jax.numpy as jnp
from jax import lax

D = 2432
HEADS = 24
HEAD = 64
PATCHES = 4
PATCH = 256
TEXT = 160
ITEMS_DEV = 4
GROUPS = 16
TEXT_PART = 40
N_REQ = 64
N_TP = 4


def draw_text_len(key, part):
    first_key, second_key = jax.random.split(jax.random.fold_in(key, 11))
    number = GROUPS * ITEMS_DEV
    base_values = jax.random.randint(first_key, (number,), 1, TEXT + 1)
    ranking = jax.random.permutation(second_key, number)
    base_values = jnp.where(ranking == 0, TEXT, base_values)
    return base_values.reshape(GROUPS, ITEMS_DEV).astype(jnp.int32)


def level_of(own_key, extent, shards, low, top_value):
    level = 1.0
    for position, parts in shards:
        draws = jax.random.uniform(jax.random.fold_in(jax.random.fold_in(own_key, 6), position), (parts,), jnp.float32, low / len(shards), top_value / len(shards))
        level = level * jnp.repeat(jnp.exp(draws), extent[position] // parts).reshape((-1,) + (1,) * (len(extent) - 1 - position))
    return level


def centred(rng, shape, scale, bound, cuts=(), held_as=jnp.bfloat16):
    loudness = level_of(rng, shape, cuts, -0.22, 0.18) if cuts else 1.0
    array = jax.random.normal(rng, shape, jnp.float32) * scale * loudness
    return jnp.minimum(jnp.maximum(array, -bound), bound).astype(held_as)


def setup_inputs(seed: int = 0) -> dict:
    key_list = jax.random.split(jax.random.key(seed), 9)
    return {
        "hidden": centred(key_list[0], (N_REQ, PATCH, ITEMS_DEV, D), 0.5, 4.0, ((0, 64),)),
        "modulation": centred(key_list[1], (GROUPS, ITEMS_DEV, 3, D), 1.0, 4.0),
        "w_qkv": centred(key_list[2], (D, 3, HEADS * HEAD), D ** -0.5, 0.125, ((2, 4),)),
        "w_out": centred(key_list[3], (HEADS * HEAD, D), HEAD ** -0.5, 0.75, ((0, 4),)),
        "qk_gain": jnp.clip(1.0 + 0.18 * jax.random.normal(key_list[4], (2, HEAD), jnp.float32), 0.1, 1.9),
        "stale_kv": centred(key_list[5], (N_REQ, PATCH, ITEMS_DEV, 2, HEADS * HEAD), 1.0, 5.0, ((0, 64), (4, 4))),
        "text_kv": centred(key_list[6], (N_REQ, TEXT_PART, ITEMS_DEV, 2, HEADS * HEAD), 1.0, 5.0, ((0, 64), (4, 4))),
        "text_len": draw_text_len(jax.random.fold_in(key_list[8], 71), 0),
    }


EPSILON = 1e-06

def modulate(rows_in, mod_rows):
    values_f = rows_in.astype(jnp.float32)
    center = values_f - lax.optimization_barrier(jnp.mean(values_f, axis=-1, keepdims=True))
    variance = lax.optimization_barrier(jnp.mean(center * center, axis=-1, keepdims=True))
    normed = center * lax.rsqrt(variance + EPSILON)
    shift_rows = mod_rows[:, 0, :].astype(jnp.float32)
    scale_rows = mod_rows[:, 1, :].astype(jnp.float32)
    return (normed * (1.0 + scale_rows) + shift_rows).astype(jnp.bfloat16)

def head_norm(heads_in, gain_row):
    square = lax.optimization_barrier(jnp.mean(heads_in * heads_in, axis=-1, keepdims=True))
    return (heads_in * lax.rsqrt(square + EPSILON) * gain_row).astype(jnp.bfloat16)

def attend(query_heads, key_heads, value_heads, valid):
    scores = jnp.einsum('rbhe,kbhe->bhrk', query_heads.astype(jnp.float32), key_heads.astype(jnp.float32)) * 0.125
    weights = jnp.exp(scores) * jnp.transpose(valid)[:, None, None, :]
    probs = (weights / lax.optimization_barrier(jnp.sum(weights, axis=-1, keepdims=True))).astype(jnp.bfloat16)
    return jnp.einsum('bhrk,kbhe->rbhe', probs.astype(jnp.float32), value_heads.astype(jnp.float32)).astype(jnp.bfloat16)

def reference(hidden, modulation, w_qkv, w_out, qk_gain, stale_kv, text_kv, text_len):
    width = HEADS * HEAD
    hidden_split = hidden.reshape(PATCHES, GROUPS, PATCH, ITEMS_DEV, D)
    stale_split = stale_kv.reshape(PATCHES, GROUPS, PATCH, ITEMS_DEV, 2, width)
    text_split = text_kv.reshape(PATCHES, GROUPS, TEXT // PATCHES, ITEMS_DEV, 2, width)
    text_pos = jnp.arange(TEXT, dtype=jnp.int32)
    w_flat = w_qkv.reshape(D, 3 * width)
    w_parts = w_out.reshape(N_TP, width // N_TP, D).astype(jnp.float32)
    patch_ids = jnp.arange(PATCHES, dtype=jnp.int32)

    def one_group(group):
        rows_in = hidden_split[:, group]
        mod_rows = modulation[group]
        modulated = modulate(rows_in, mod_rows)
        projections = jnp.dot(modulated.reshape(-1, D), w_flat, preferred_element_type=jnp.float32)
        projections = projections.reshape(PATCHES, PATCH, ITEMS_DEV, 3, HEADS, HEAD)
        query_heads = head_norm(projections[:, :, :, 0], qk_gain[0])
        key_heads = head_norm(projections[:, :, :, 1], qk_gain[1])
        value_heads = projections[:, :, :, 2].astype(jnp.bfloat16)
        fresh_pairs = jnp.stack([key_heads.reshape(PATCHES, PATCH, ITEMS_DEV, width), value_heads.reshape(PATCHES, PATCH, ITEMS_DEV, width)], axis=3)
        text_pairs = text_split[:, group].reshape(TEXT, ITEMS_DEV, 2, width)
        text_valid = (text_pos[:, None] < text_len[group][None, :]).astype(jnp.float32)
        valid = jnp.concatenate([jnp.ones((PATCHES * PATCH, ITEMS_DEV), jnp.float32), text_valid], axis=0)
        gate_rows = mod_rows[:, 2, :].astype(jnp.float32)
        results = []
        for patch in range(PATCHES):
            own_patch = (patch_ids == patch)[:, None, None, None, None]
            image_pairs = jnp.where(own_patch, fresh_pairs, stale_split[:, group])
            image_pairs = image_pairs.reshape(PATCHES * PATCH, ITEMS_DEV, 2, width)
            all_pairs = jnp.concatenate([image_pairs, text_pairs], axis=0)
            all_keys = all_pairs[:, :, 0].reshape(-1, ITEMS_DEV, HEADS, HEAD)
            all_values = all_pairs[:, :, 1].reshape(-1, ITEMS_DEV, HEADS, HEAD)
            mixed = attend(query_heads[patch], all_keys, all_values, valid)
            mixed = mixed.reshape(PATCH, ITEMS_DEV, N_TP, width // N_TP)
            partial_terms = jnp.einsum('rbge,ged->grbd', mixed.astype(jnp.float32), w_parts).astype(jnp.bfloat16)
            partial_terms = lax.optimization_barrier(partial_terms)
            attn = lax.optimization_barrier(jnp.sum(partial_terms.astype(jnp.float32), axis=0))
            results.append((rows_in[patch].astype(jnp.float32) + gate_rows[None] * attn).astype(jnp.bfloat16))
        return (jnp.stack(results), fresh_pairs)
    updated, fresh_all = lax.map(one_group, jnp.arange(GROUPS, dtype=jnp.int32))
    updated = jnp.transpose(updated, (1, 0, 2, 3, 4)).reshape(N_REQ, PATCH, ITEMS_DEV, D)
    fresh_all = jnp.transpose(fresh_all, (1, 0, 2, 3, 4, 5)).reshape(N_REQ, PATCH, ITEMS_DEV, 2, width)
    return (updated, fresh_all)
```

```python
import functools

import jax
import jax.numpy as jnp
from jax import lax
from jax.experimental import pallas as pl
from jax.experimental.pallas import tpu as pltpu
from jax.sharding import PartitionSpec as P

HEAD = 64
PATCHES = 4
EPSILON = 1e-06
LANES = 128
BF = jnp.bfloat16
F32 = jnp.float32
NT = (((1,), (1,)), ((), ()))
COST = pl.CostEstimate(flops=1000, bytes_accessed=1000, transcendentals=0)


def dot(a, b):
    return jnp.dot(a, b, preferred_element_type=F32)


def params(limit_mb, **kw):
    return pltpu.CompilerParams(vmem_limit_bytes=limit_mb << 20, **kw)


def split_bf(value):
    high = value.astype(BF)
    return high, (value - high.astype(F32)).astype(BF)


def block_ones(rows):
    a = lax.broadcasted_iota(jnp.int32, (rows, LANES), 0) % LANES // HEAD
    b = lax.broadcasted_iota(jnp.int32, (rows, LANES), 1) // HEAD
    return (a == b).astype(F32).astype(BF)


def pack_kernel(item_ref, stale_ref, text_ref, out_ref):
    rows = stale_ref.shape[0]
    for j in range(2):
        out_ref[j, 0:rows] = stale_ref[:, j, :]
        out_ref[j, rows:] = text_ref[:, j, :]


def pack(item, stale, text):
    rows, _, _, width = stale.shape
    trows = text.shape[0]
    grid_spec = pltpu.PrefetchScalarGridSpec(
        num_scalar_prefetch=1,
        grid=(1,),
        in_specs=[
            pl.BlockSpec((rows, None, 2, width), lambda s, it: (0, it[0], 0, 0)),
            pl.BlockSpec((trows, None, 2, width), lambda s, it: (0, it[0], 0, 0)),
        ],
        out_specs=pl.BlockSpec((2, rows + trows, width), lambda s, it: (0, 0, 0)),
    )
    return pl.pallas_call(
        pack_kernel,
        grid_spec=grid_spec,
        out_shape=jax.ShapeDtypeStruct((2, rows + trows, width), BF),
        compiler_params=params(58),
        cost_estimate=COST,
        name="pack",
    )(item, stale, text)


def project_kernel(s_ref, hidden_hbm, mod_ref, gain_ref, w_hbm, q_ref, k_ref, v_ref, *scratch):
    w_ref, h_ref, xa_ref, xb_ref, scale_ref, shift_ref, y_ref, sems = scratch
    outs = (q_ref, k_ref, v_ref)
    blocks, rows, items, width_d = h_ref.shape
    width = w_hbm.shape[2]
    tiles = width // LANES
    loads = [
        pltpu.make_async_copy(hidden_hbm.at[pl.ds(b * rows, rows)], h_ref.at[b], sems.at[b]) for b in range(blocks)
    ]
    weights = [
        pltpu.make_async_copy(w_hbm.at[j], w_ref.at[:, pl.ds(j * width, width)], sems.at[blocks + j]) for j in range(3)
    ]
    loads[0].start()
    for copy in weights:
        copy.start()
    for copy in loads[1:]:
        copy.start()
    shift = mod_ref[0].astype(F32)
    scale = 1.0 + mod_ref[1].astype(F32)
    shift_ref[...] = jnp.concatenate([shift, shift], axis=0)
    scale_ref[...] = jnp.concatenate([scale, scale], axis=0)
    wide = 2 * LANES
    r = lax.broadcasted_iota(jnp.int32, (2 * wide, wide), 0) % wide // HEAD
    c = lax.broadcasted_iota(jnp.int32, (2 * wide, wide), 1) // HEAD
    ones = (r == c).astype(F32).astype(BF)

    def norm_rows(block, x_ref, c):
        x = h_ref[block, c * 4 : c * 4 + 4].reshape(16, width_d).astype(F32).reshape(2, 8, width_d)
        center = x - jnp.mean(x, axis=-1, keepdims=True)
        variance = jnp.mean(center * center, axis=-1, keepdims=True)
        normed = center * lax.rsqrt(variance + EPSILON)
        out = normed * scale_ref[...][None] + shift_ref[...][None]
        x_ref[c * 16 : c * 16 + 16, :] = out.reshape(16, width_d).astype(BF)

    def finish_tile(block, n, y):
        if n + wide <= 2 * width:
            high, low = split_bf(y * y)
            square = dot(jnp.concatenate([high, low], axis=1), ones) * (1.0 / HEAD)
            y = y * lax.rsqrt(square + EPSILON) * gain_ref[:, n : n + wide]
        for t in range(y.shape[1] // LANES):
            tile = n // LANES + t
            j = tile // tiles
            y_ref[tile] = y[:, t * LANES : (t + 1) * LANES]
            where = slice(block * rows, (block + 1) * rows)
            to = slice(tile % tiles * LANES, (tile % tiles + 1) * LANES)
            for i in range(items):
                outs[j][i, where, to] = y_ref[tile, pl.ds(i, rows, stride=items), :].astype(BF)

    chunks = rows // 4
    pending = []
    for block in range(blocks + 1):
        now, later = (xb_ref, xa_ref) if block % 2 == 0 else (xa_ref, xb_ref)
        if block < blocks:
            loads[block].wait()
        if block == 0:
            for c in range(chunks):
                norm_rows(0, later, c)
            for copy in weights:
                copy.wait()
            continue
        starts = list(range(0, 3 * width, wide))
        for at, n in enumerate(starts):
            y = dot(now[...], w_ref[:, n : min(n + wide, 3 * width)])
            if block < blocks:
                for c in range(at * chunks // len(starts), (at + 1) * chunks // len(starts)):
                    norm_rows(block, later, c)
            if pending:
                finish_tile(*pending.pop())
            pending.append((block - 1, n, y))
    finish_tile(*pending.pop())


def project(scalars, hidden, modulation, gains, w):
    row_total, items, width_d = hidden.shape
    width = w.shape[2]
    rows = 128
    blocks = row_total // rows
    out = pl.BlockSpec((items, row_total, width), lambda s, r: (0, 0, 0))
    grid_spec = pltpu.PrefetchScalarGridSpec(
        num_scalar_prefetch=1,
        grid=(1,),
        in_specs=[
            pl.BlockSpec(memory_space=pl.ANY),
            pl.BlockSpec((None, 3, items, width_d), lambda s, r: (r[4], 0, 0, 0)),
            pl.BlockSpec((1, 2 * width), lambda s, r: (0, 0)),
            pl.BlockSpec(memory_space=pl.ANY),
        ],
        out_specs=[out] * 3,
        scratch_shapes=[
            pltpu.VMEM((width_d, 3 * width), BF),
            pltpu.VMEM((blocks, rows, items, width_d), BF),
            pltpu.VMEM((rows * items, width_d), BF),
            pltpu.VMEM((rows * items, width_d), BF),
            pltpu.VMEM((8, width_d), F32),
            pltpu.VMEM((8, width_d), F32),
            pltpu.VMEM((3 * width // LANES, rows * items, LANES), F32),
            pltpu.SemaphoreType.DMA((blocks + 3,)),
        ],
    )
    return pl.pallas_call(
        project_kernel,
        grid_spec=grid_spec,
        out_shape=[jax.ShapeDtypeStruct((items, row_total, width), BF)] * 3,
        compiler_params=params(58),
        cost_estimate=COST,
        name="project",
    )(scalars, hidden, modulation, gains, w)


def half_masks():
    lane = lax.broadcasted_iota(jnp.int32, (8, LANES), 1)
    return [(lane < HEAD).astype(F32)[0:1].astype(BF), (lane >= HEAD).astype(F32)[0:1].astype(BF)]


def weigh(values, mask, valid=None):
    ones = jnp.broadcast_to(mask, values.shape)
    both = jnp.concatenate([values * mask, ones], axis=1)
    return both if valid is None else both * valid


def sums_tile(sums):
    rows = sums.shape[0]
    r = lax.broadcasted_iota(jnp.int32, (rows, LANES), 0)
    c = lax.broadcasted_iota(jnp.int32, (rows, LANES), 1) % HEAD
    line = jnp.sum(jnp.where(r == c, sums, 0.0), axis=0, keepdims=True)
    high = line.astype(BF).astype(F32)
    low = line - high
    at = lax.broadcasted_iota(jnp.int32, (8, LANES), 0)
    return jnp.where(at == 0, high, jnp.where(at == 1, low, 0.0)).astype(BF)


def own_kernel(s_ref, q_ref, k_ref, v_ref, *refs):
    out_refs, part_ref, sums_ref = refs[:PATCHES], refs[PATCHES], refs[PATCHES + 1]
    rows, width = q_ref.shape
    share = rows // PATCHES
    masks = half_masks()
    for t in range(width // LANES):
        lanes = slice(t * LANES, (t + 1) * LANES)
        kp, vp, qp = k_ref[:, lanes], v_ref[:, lanes], q_ref[:, lanes]
        acc = None
        for h in range(2):
            p = jnp.exp(lax.dot_general(qp * masks[h], kp, NT, preferred_element_type=F32)).astype(BF)
            term = dot(p, weigh(vp, masks[h]))
            acc = term if acc is None else acc + term
        sums = acc[:, LANES:]
        sums_ref[t] = sums
        part_ref[t] = acc[:, :LANES] / sums
        for g in range(PATCHES):
            at = pl.ds(pl.multiple_of((s_ref[7] ^ g) * share, share), share)
            out_refs[g][0:share, lanes] = part_ref[t, at, :].astype(BF)
            out_refs[g][share : share + 8, lanes] = sums_tile(sums_ref[t, at, :])


def own_attention(scalars, q, k, v):
    items, rows, width = k.shape
    share = rows // PATCHES
    grid_spec = pltpu.PrefetchScalarGridSpec(
        num_scalar_prefetch=1,
        grid=(items,),
        in_specs=[pl.BlockSpec((None, rows, width), lambda s, r: (s, 0, 0))] * 3,
        out_specs=[pl.BlockSpec((None, share + 8, width), lambda s, r: (s, 0, 0))] * PATCHES,
        scratch_shapes=[pltpu.VMEM((width // LANES, rows, LANES), F32)] * 2,
    )
    return pl.pallas_call(
        own_kernel,
        grid_spec=grid_spec,
        out_shape=[jax.ShapeDtypeStruct((items, share + 8, width), BF)] * PATCHES,
        compiler_params=params(58),
        cost_estimate=COST,
        name="own",
    )(scalars, q, k, v)


def remote_kernel(s_ref, *refs):
    q_refs, kv_refs = refs[0:PATCHES], refs[PATCHES : 2 * PATCHES]
    out_ref, w_ref, text_ref = refs[2 * PATCHES :]
    rows = q_refs[0].shape[0]
    trows = kv_refs[0].shape[1] - rows
    share = rows // PATCHES
    patch, length = s_ref[5], s_ref[6]
    masks = half_masks()
    text_ref[...] = jnp.zeros_like(text_ref)
    position = lax.broadcasted_iota(jnp.int32, (rows, 2 * LANES), 0)
    good = position < 0
    for o in range(PATCHES):
        for j in range(2):
            text_ref[j, o * trows : (o + 1) * trows] = kv_refs[o][j, rows:].astype(F32)
        owner = lax.rem(patch - o + PATCHES, PATCHES)
        here = (position >= o * trows) & (position < (o + 1) * trows)
        good = good | (here & (position - o * trows + owner * trows < length))
    valid = good.astype(F32).astype(BF)
    text_k, text_v = text_ref[0].astype(BF), text_ref[1].astype(BF)
    for h in range(2):
        for o in range(PATCHES):
            w_ref[h, o] = weigh(kv_refs[o][1, 0:rows], masks[h])
        w_ref[h, PATCHES] = weigh(text_v, masks[h], valid)
    for o in range(PATCHES):
        qp = q_refs[o][...]
        acc = None
        for h in range(2):
            qh = qp * masks[h]
            for c in range(PATCHES + 1):
                if c == o:
                    continue
                keys = text_k if c == PATCHES else kv_refs[c][0, 0:rows]
                p = jnp.exp(lax.dot_general(qh, keys, NT, preferred_element_type=F32)).astype(BF)
                term = dot(p, w_ref[h, c])
                acc = term if acc is None else acc + term
        sums = acc[:, LANES:]
        part = (acc[:, :LANES] / sums).astype(BF)
        base = lax.rem(patch - o + PATCHES, PATCHES) * PATCHES
        for u in range(PATCHES):
            out_ref[base + u, 0:share] = part[u * share : (u + 1) * share]
            out_ref[base + u, share : share + 8] = sums_tile(sums[u * share : (u + 1) * share])


def remote_attention(scalars, q, far_qs, kvs):
    _, rows, width = q.shape
    total = kvs[0].shape[1]
    share = rows // PATCHES
    grid_spec = pltpu.PrefetchScalarGridSpec(
        num_scalar_prefetch=1,
        grid=(width // LANES,),
        in_specs=[pl.BlockSpec((None, rows, LANES), lambda s, r: (r[5], 0, s))]
        + [pl.BlockSpec((rows, LANES), lambda s, r: (0, s))] * (PATCHES - 1)
        + [pl.BlockSpec((2, total, LANES), lambda s, r: (0, 0, s))] * PATCHES,
        out_specs=pl.BlockSpec((PATCHES * PATCHES, share + 8, LANES), lambda s, r: (0, 0, s)),
        scratch_shapes=[
            pltpu.VMEM((2, PATCHES + 1, rows, 2 * LANES), BF),
            pltpu.VMEM((2, rows, LANES), F32),
        ],
    )
    return pl.pallas_call(
        remote_kernel,
        grid_spec=grid_spec,
        out_shape=jax.ShapeDtypeStruct((PATCHES * PATCHES, share + 8, width), BF),
        compiler_params=params(58),
        cost_estimate=COST,
        name="remote",
    )(scalars, q, *far_qs, *kvs)


def spread(lines, ones2):
    r = lax.broadcasted_iota(jnp.int32, (HEAD, LANES), 0)
    c = lax.broadcasted_iota(jnp.int32, (HEAD, LANES), 1) % HEAD
    parts = []
    for line in lines:
        f = line.astype(F32)
        parts.append(
            jnp.concatenate(
                [jnp.where(r == c, f[0:1], 0.0), jnp.where(r == c, f[1:2], 0.0)], axis=1
            ).astype(BF)
        )
    return dot(jnp.concatenate(parts, axis=0), ones2)


def finish_kernel(s_ref, far_ref, near0, near1, near2, near3, hidden_ref, mod_ref, w0, w1, w2, w3, out_ref, acc_ref):
    nears, ws = [near0, near1, near2, near3], [w0, w1, w2, w3]
    share, items, width_d = hidden_ref.shape
    rows = share * items
    width = w0.shape[0]
    ones2 = block_ones(2 * LANES)
    a = lax.broadcasted_iota(jnp.int32, (rows, rows), 0)
    b = lax.broadcasted_iota(jnp.int32, (rows, rows), 1)
    order = ((a % items) * share + a // items == b).astype(F32).astype(BF)
    tp = s_ref[7]
    for g in range(4):
        source = tp ^ g
        mixed = []
        for t in range(width // LANES):
            lanes = slice(t * LANES, (t + 1) * LANES)
            far = [far_ref[i, source, :, lanes] for i in range(items)]
            near = [nears[g][i, :, lanes] for i in range(items)]
            sums = [spread([x[share:] for x in part], ones2) for part in (far, near)]
            values = [
                jnp.concatenate([x[:share] for x in part], axis=0).astype(F32) for part in (far, near)
            ]
            total = values[0] * sums[0] + values[1] * sums[1]
            mixed.append((total / (sums[0] + sums[1])).astype(BF))
        joined = dot(order, jnp.concatenate(mixed, axis=1)).astype(BF)
        for n in range(0, width_d, 256):
            lanes = slice(n, min(n + 256, width_d))
            term = dot(joined, ws[g][:, lanes]).astype(BF).astype(F32)
            if g == 0:
                acc_ref[:, lanes] = term
            else:
                acc_ref[:, lanes] += term
    gate = mod_ref[2].astype(F32)
    gate = jnp.concatenate([gate, gate], axis=0)

    def last(c, carry):
        at = pl.multiple_of(c * 16, 16)
        own = hidden_ref[pl.ds(c * 4, 4)].reshape(16, width_d).astype(F32).reshape(2, 8, width_d)
        new = own + gate[None] * acc_ref[pl.ds(at, 16), :].reshape(2, 8, width_d)
        out_ref[pl.ds(c * 4, 4)] = new.reshape(16, width_d).astype(BF).reshape(4, items, width_d)
        return carry

    lax.fori_loop(0, rows // 16, last, 0, unroll=4)


def finish(scalars, far, near, hidden, modulation, ws):
    row_total, items, width_d = hidden.shape
    share = row_total // PATCHES
    width = ws[0].shape[0]
    grid_spec = pltpu.PrefetchScalarGridSpec(
        num_scalar_prefetch=1,
        grid=(1,),
        in_specs=[pl.BlockSpec((items, 4, share + 8, width), lambda s, r: (0, 0, 0, 0))]
        + [pl.BlockSpec((items, share + 8, width), lambda s, r: (0, 0, 0))] * 4
        + [
            pl.BlockSpec((share, items, width_d), lambda s, r: (r[7], 0, 0)),
            pl.BlockSpec((None, 3, items, width_d), lambda s, r: (r[4], 0, 0, 0)),
        ]
        + [pl.BlockSpec(memory_space=pltpu.VMEM)] * 4,
        out_specs=pl.BlockSpec((share, items, width_d), lambda s, r: (0, 0, 0)),
        scratch_shapes=[
            pltpu.VMEM((share * items, width_d), F32),
        ],
    )
    return pl.pallas_call(
        finish_kernel,
        grid_spec=grid_spec,
        out_shape=jax.ShapeDtypeStruct((share, items, width_d), BF),
        compiler_params=params(58),
        cost_estimate=COST,
        name="finish",
    )(scalars, far, *near, hidden, modulation, *ws)


def body(layout, hidden, modulation, w_qkv, w_out, qk_gain, stale_kv, text_kv, text_len):
    slots, tps, groups, w_pairs, core_pairs = layout
    place = lax.axis_index("req")
    tp = lax.axis_index("tp")
    group = place % groups
    patch = place // groups
    items_at = [(patch + o) % PATCHES for o in range(PATCHES)]
    length = lax.dynamic_slice(text_len, (group, patch), (1, 1))[0, 0]
    scalars = jnp.stack([v.astype(jnp.int32) for v in items_at + [group, patch, length, tp]])
    both = ("req", "tp")
    local_heads = w_out.shape[0] // HEAD

    columns = [[g + groups * p for p in range(PATCHES)] for g in range(groups)]
    rings = [[place * tps + t for place in column for t in range(tps)] for column in columns]

    def along_x(value, by):
        return lax.ppermute(value, "req", [(i, (i + by * groups) % slots) for i in range(slots)])

    packed = [pack(items_at[o].astype(jnp.int32)[None], stale_kv[0], text_kv[0]) for o in range(PATCHES)]
    *packed, scalars = lax.optimization_barrier((*packed, scalars))
    kvs = [packed[0]] + [along_x(packed[o], o) for o in (1, 2, 3)]
    w_far = lax.ppermute(w_out, both, w_pairs)
    w_near = lax.ppermute(w_out, both, core_pairs)
    mod = jnp.transpose(modulation, (0, 2, 1, 3))
    gains = jnp.concatenate([qk_gain[0] * 0.125] * local_heads + [qk_gain[1]] * local_heads)[None]
    q, k, v = project(scalars, hidden[0], mod, gains, jnp.transpose(w_qkv, (1, 0, 2)))
    owns = own_attention(scalars, q, k, v)
    pieces = [lax.dynamic_index_in_dim(q, items_at[o], 0, keepdims=False) for o in range(1, PATCHES)]
    pieces, kvs, owns = lax.optimization_barrier((pieces, kvs, owns))
    far_qs = [along_x(pieces[o - 1], o) for o in range(1, PATCHES)]
    w_across = lax.ppermute(w_far, both, core_pairs)
    near = [owns[0]] + [
        lax.ppermute(owns[g], "tp", [(i, i ^ g) for i in range(tps)]) for g in range(1, tps)
    ]
    sent = remote_attention(scalars, q, far_qs, kvs)
    far = lax.all_to_all(sent, both, 0, 0, axis_index_groups=rings, tiled=True)
    far = far.reshape(PATCHES, tps, *far.shape[1:])
    fresh = jnp.transpose(jnp.stack([k, v], axis=0), (2, 1, 0, 3))
    updated = finish(scalars, far, near, hidden[0], mod, [w_out, w_near, w_far, w_across])
    return (updated[None], fresh[None])


def solution(mesh):
    slots, tps = mesh.shape["req"], mesh.shape["tp"]
    groups = slots // PATCHES
    ring = 8
    w_pairs = []
    for place in range(slots):
        column, high = place // (ring // 2), place % (ring // 2)
        for t in range(tps):
            low, core = t // 2, t % 2
            z = (2 * high + low + (1 if core else -1)) % ring
            target = column * (ring // 2) + z // 2
            w_pairs.append((place * tps + t, target * tps + z % 2 * 2 + core))
    core_pairs = [(i, i ^ 1) for i in range(slots * tps)]
    layout = (slots, tps, groups, w_pairs, core_pairs)
    return jax.shard_map(
        functools.partial(body, layout),
        mesh=mesh,
        in_specs=(
            P("req", None, None, None),
            P(),
            P(None, None, "tp"),
            P("tp", None),
            P(),
            P("req", None, None, None, "tp"),
            P("req", None, None, None, "tp"),
            P(),
        ),
        out_specs=(P("req", "tp", None, None), P("req", None, None, None, "tp")),
        check_vma=False,
    )
```

```python
import functools

import jax
import jax.numpy as jnp
from jax import lax
from jax.experimental import pallas as pl
from jax.experimental.pallas import tpu as pltpu
from jax.sharding import PartitionSpec as P

HEAD = 64
PATCHES = 4
EPSILON = 1e-06
LANES = 128
BF = jnp.bfloat16
F32 = jnp.float32
NT = (((1,), (1,)), ((), ()))
COST = pl.CostEstimate(flops=1000, bytes_accessed=1000, transcendentals=0)


def dot(a, b):
    return jnp.dot(a, b, preferred_element_type=F32)


def params(limit_mb, **kw):
    return pltpu.CompilerParams(vmem_limit_bytes=limit_mb << 20, **kw)


def split_bf(value):
    high = value.astype(BF)
    return high, (value - high.astype(F32)).astype(BF)


def block_ones(rows):
    a = lax.broadcasted_iota(jnp.int32, (rows, LANES), 0) % LANES // HEAD
    b = lax.broadcasted_iota(jnp.int32, (rows, LANES), 1) // HEAD
    return (a == b).astype(F32).astype(BF)


def project_kernel(s_ref, hidden_hbm, mod_ref, gain_ref, w_hbm, text_ref, q_hbm, k_ref, v_ref, *scratch):
    q_ref, hidden_ref, w_ref, xa_ref, xb_ref, scale_ref, shift_ref, y_ref, sems = scratch
    rows = xa_ref.shape[0] // hidden_ref.shape[1]
    blocks = hidden_ref.shape[0] // rows
    items, width_d = hidden_ref.shape[1:]
    loads = [
        pltpu.make_async_copy(
            hidden_hbm.at[pl.ds(b * rows, rows)], hidden_ref.at[pl.ds(b * rows, rows)], sems.at[b]
        )
        for b in range(blocks)
    ]
    columns = w_hbm.shape[2]
    weights = [
        pltpu.make_async_copy(w_hbm.at[j], w_ref.at[:, pl.ds(j * columns, columns)], sems.at[blocks + j])
        for j in range(3)
    ]
    send = pltpu.make_async_copy(q_ref, q_hbm, sems.at[blocks + 3])
    for load in loads[:1] + weights + loads[1:]:
        load.start()
    trows = text_ref.shape[0]
    total = hidden_ref.shape[0]
    for i in range(items):
        for j in range(2):
            q_ref[i, total + j * trows : total + (j + 1) * trows] = text_ref[:, i, j, :]
    width = w_hbm.shape[2]
    tiles = width // LANES
    gain = gain_ref[...]
    gains = jnp.concatenate(
        [gain[0:1] * 0.125] * (width // HEAD) + [gain[1:2]] * (width // HEAD), axis=1
    )
    shift = mod_ref[0].astype(F32)
    scale = 1.0 + mod_ref[1].astype(F32)
    shift_ref[...] = jnp.concatenate([shift, shift], axis=0)
    scale_ref[...] = jnp.concatenate([scale, scale], axis=0)
    wide = 2 * LANES
    r = lax.broadcasted_iota(jnp.int32, (2 * wide, wide), 0) % wide // HEAD
    c = lax.broadcasted_iota(jnp.int32, (2 * wide, wide), 1) // HEAD
    ones = (r == c).astype(F32).astype(BF)

    def norm_rows(block, x_ref, c):
        first = block * rows + c * 4
        x = hidden_ref[first : first + 4].reshape(16, width_d).astype(F32).reshape(2, 8, width_d)
        center = x - jnp.mean(x, axis=-1, keepdims=True)
        variance = jnp.mean(center * center, axis=-1, keepdims=True)
        normed = center * lax.rsqrt(variance + EPSILON)
        out = normed * scale_ref[...][None] + shift_ref[...][None]
        x_ref[c * 16 : c * 16 + 16, :] = out.reshape(16, width_d).astype(BF)

    def finish_tile(block, n, y):
        if n + wide <= 2 * width:
            high, low = split_bf(y * y)
            square = dot(jnp.concatenate([high, low], axis=1), ones) * (1.0 / HEAD)
            y = y * lax.rsqrt(square + EPSILON) * gains[:, n : n + wide]
        for t in range(y.shape[1] // LANES):
            tile = n // LANES + t
            j = tile // tiles
            y_ref[tile] = y[:, t * LANES : (t + 1) * LANES]
            where = slice(block * rows, (block + 1) * rows)
            to = slice(tile % tiles * LANES, (tile % tiles + 1) * LANES)
            for i in range(items):
                (q_ref, k_ref, v_ref)[j][i, where, to] = y_ref[tile, pl.ds(i, rows, stride=items), :].astype(BF)

    chunks = rows // 4
    pending = []
    for block in range(blocks + 1):
        now, later = (xb_ref, xa_ref) if block % 2 == 0 else (xa_ref, xb_ref)
        if block < blocks:
            loads[block].wait()
        if block == 0:
            for c in range(chunks):
                norm_rows(0, later, c)
            for load in weights:
                load.wait()
            continue
        starts = list(range(0, 3 * width, wide))
        for at, n in enumerate(starts):
            y = dot(now[...], w_ref[:, n : min(n + wide, 3 * width)])
            if block < blocks:
                for c in range(at * chunks // len(starts), (at + 1) * chunks // len(starts)):
                    norm_rows(block, later, c)
            if pending:
                done = pending.pop()
                finish_tile(*done)
                if done[0] == blocks - 1 and done[1] < width <= done[1] + wide:
                    send.start()
            pending.append((block - 1, n, y))
    finish_tile(*pending.pop())
    send.wait()


def project(scalars, hidden, modulation, gains, w, text):
    row_total, items, width_d = hidden.shape
    width = w.shape[2]
    rows = 64
    q_rows = row_total + 2 * text.shape[0]
    vmem = pl.BlockSpec(memory_space=pltpu.VMEM)
    grid_spec = pltpu.PrefetchScalarGridSpec(
        num_scalar_prefetch=1,
        grid=(1,),
        in_specs=[
            pl.BlockSpec(memory_space=pltpu.HBM),
            pl.BlockSpec((None, 3, items, width_d), lambda s, r: (r[4], 0, 0, 0)),
            vmem,
            pl.BlockSpec(memory_space=pltpu.HBM),
            vmem,
        ],
        out_specs=[pl.BlockSpec(memory_space=pltpu.HBM)] + [vmem] * 2,
        scratch_shapes=[
            pltpu.VMEM((items, q_rows, width), BF),
            pltpu.VMEM((row_total, items, width_d), BF),
            pltpu.VMEM((width_d, 3 * width), BF),
            pltpu.VMEM((rows * items, width_d), BF),
            pltpu.VMEM((rows * items, width_d), BF),
            pltpu.VMEM((8, width_d), F32),
            pltpu.VMEM((8, width_d), F32),
            pltpu.VMEM((3 * width // LANES, rows * items, LANES), F32),
            pltpu.SemaphoreType.DMA((row_total // rows + 4,)),
        ],
    )
    return pl.pallas_call(
        project_kernel,
        grid_spec=grid_spec,
        out_shape=[jax.ShapeDtypeStruct((items, q_rows, width), BF)]
        + [jax.ShapeDtypeStruct((items, row_total, width), BF)] * 2,
        compiler_params=params(60),
        cost_estimate=COST,
        name="project",
    )(scalars, hidden, modulation, gains, w, text)


def half_masks():
    lane = lax.broadcasted_iota(jnp.int32, (8, LANES), 1)
    return [(lane < HEAD).astype(F32)[0:1].astype(BF), (lane >= HEAD).astype(F32)[0:1].astype(BF)]


def weigh(values, mask, valid=None):
    ones = jnp.broadcast_to(mask, values.shape)
    both = jnp.concatenate([values * mask, ones], axis=1)
    return both if valid is None else both * valid


def sums_tiles(sums, share):
    count = sums.shape[0] // share
    r = lax.broadcasted_iota(jnp.int32, (share, LANES), 0)
    c = lax.broadcasted_iota(jnp.int32, (share, LANES), 1) % HEAD
    own = (r == c).astype(F32)
    at = lax.broadcasted_iota(jnp.int32, (8, LANES), 0)
    tiles = []
    for u in range(count):
        line = jnp.sum(sums[u * share : (u + 1) * share] * own, axis=0, keepdims=True)
        high = line.astype(BF).astype(F32)
        tiles.append(jnp.where(at == 0, high, jnp.where(at == 1, line - high, 0.0)).astype(BF))
    return tiles


def own_kernel(s_ref, q_ref, k_ref, v_ref, *refs):
    out_refs, part_ref, sems = refs[:PATCHES], refs[PATCHES], refs[PATCHES + 1]
    items, rows, width = k_ref.shape
    share = rows // PATCHES
    masks = half_masks()
    for i in range(items):
        for t in range(width // LANES):
            lanes = slice(t * LANES, (t + 1) * LANES)
            kp, vp, qp = k_ref[i, :, lanes], v_ref[i, :, lanes], q_ref[i, 0:rows, lanes]
            ps = [
                jnp.exp(lax.dot_general(qp * mask, kp, NT, preferred_element_type=F32)).astype(BF)
                for mask in masks
            ]
            acc = dot(
                jnp.concatenate(ps, axis=1), jnp.concatenate([weigh(vp, mask) for mask in masks], axis=0)
            )
            sums = acc[:, LANES:]
            part = (acc[:, :LANES] / sums).astype(BF)
            for u, tile in enumerate(sums_tiles(sums, share)):
                part_ref[u, i, 0:share, lanes] = part[u * share : (u + 1) * share]
                part_ref[u, i, share : share + 8, lanes] = tile
    copies = [
        pltpu.make_async_copy(part_ref.at[s_ref[6] ^ g], out_refs[g], sems.at[g]) for g in range(PATCHES)
    ]
    for copy in copies:
        copy.start()
    for copy in copies:
        copy.wait()


def own_attention(scalars, q, k, v):
    items, rows, width = k.shape
    share = rows // PATCHES
    vmem = pl.BlockSpec(memory_space=pltpu.VMEM)
    return pl.pallas_call(
        own_kernel,
        in_specs=[pl.BlockSpec(memory_space=pltpu.SMEM)] + [vmem] * 3,
        out_specs=[pl.BlockSpec(memory_space=pltpu.HBM)] * PATCHES,
        out_shape=[jax.ShapeDtypeStruct((items, share + 8, width), BF)] * PATCHES,
        scratch_shapes=[
            pltpu.VMEM((PATCHES, items, share + 8, width), BF),
            pltpu.SemaphoreType.DMA((PATCHES,)),
        ],
        compiler_params=params(60),
        cost_estimate=COST,
        name="own",
    )(scalars, q, k, v)


def remote_kernel(s_ref, length_ref, *refs):
    q_all, kv_refs = refs[0], refs[1 : 1 + PATCHES]
    out_ref, text_ref = refs[1 + PATCHES :]
    rows = kv_refs[0].shape[0]
    trows = (q_all.shape[1] - rows) // 2
    share = rows // PATCHES
    group, patch = s_ref[4], s_ref[5]
    q_refs = [q_all.at[lax.rem(patch - o + PATCHES, PATCHES)] for o in range(PATCHES)]
    length = length_ref[patch, group]
    masks = half_masks()
    text_ref[...] = jnp.zeros_like(text_ref)
    good = lax.broadcasted_iota(jnp.int32, (rows, 2 * LANES), 0) < length
    for p in range(PATCHES):
        for j in range(2):
            first = rows + j * trows
            text_ref[j, p * trows : (p + 1) * trows] = q_all[p, first : first + trows].astype(F32)
    valid = good.astype(F32).astype(BF)
    text_k, text_v = text_ref[0].astype(BF), text_ref[1].astype(BF)
    accs = [None] * PATCHES
    for c in range(PATCHES + 1):
        if c == PATCHES:
            keys, values = text_k, [weigh(text_v, mask, valid) for mask in masks]
        else:
            pair = kv_refs[c]
            keys, values = pair[:, 0, :], pair[:, 1, :]
            values = [weigh(values, mask) for mask in masks]
        which = [o for o in range(PATCHES) if o != c]
        queries = jnp.concatenate([q_refs[o][0:rows] for o in which], axis=0)
        ps = [
            jnp.exp(lax.dot_general(queries * mask, keys, NT, preferred_element_type=F32)).astype(BF)
            for mask in masks
        ]
        term = dot(jnp.concatenate(ps, axis=1), jnp.concatenate(values, axis=0))
        for at, o in enumerate(which):
            piece = term[at * rows : (at + 1) * rows]
            accs[o] = piece if accs[o] is None else accs[o] + piece
    for o in range(PATCHES):
        sums = accs[o][:, LANES:]
        part = (accs[o][:, :LANES] / sums).astype(BF)
        base = lax.rem(patch - o + PATCHES, PATCHES) * PATCHES
        for u, tile in enumerate(sums_tiles(sums, share)):
            out_ref[base + u, 0:share] = part[u * share : (u + 1) * share]
            out_ref[base + u, share : share + 8] = tile


def remote_attention(scalars, lengths, q, stale, kvs):
    rows, _, _, width = stale.shape
    q_rows = q.shape[1]
    share = rows // PATCHES
    grid_spec = pltpu.PrefetchScalarGridSpec(
        num_scalar_prefetch=2,
        grid=(width // LANES,),
        in_specs=[pl.BlockSpec((PATCHES, q_rows, LANES), lambda s, r, t: (0, 0, s))]
        + [pl.BlockSpec((rows, None, 2, LANES), lambda s, r, t: (0, r[0], 0, s))]
        + [pl.BlockSpec((rows, 2, LANES), lambda s, r, t: (0, 0, s))] * (PATCHES - 1),
        out_specs=pl.BlockSpec((PATCHES * PATCHES, share + 8, LANES), lambda s, r, t: (0, 0, s)),
        scratch_shapes=[pltpu.VMEM((2, rows, LANES), F32)],
    )
    return pl.pallas_call(
        remote_kernel,
        grid_spec=grid_spec,
        out_shape=jax.ShapeDtypeStruct((PATCHES * PATCHES, share + 8, width), BF),
        compiler_params=params(60),
        cost_estimate=COST,
        name="remote",
    )(scalars, lengths, q, stale, *kvs)


def spread(lines, ones2):
    r = lax.broadcasted_iota(jnp.int32, (HEAD, LANES), 0)
    c = lax.broadcasted_iota(jnp.int32, (HEAD, LANES), 1) % HEAD
    parts = []
    for line in lines:
        f = line.astype(F32)
        parts.append(
            jnp.concatenate(
                [jnp.where(r == c, f[0:1], 0.0), jnp.where(r == c, f[1:2], 0.0)], axis=1
            ).astype(BF)
        )
    return dot(jnp.concatenate(parts, axis=0), ones2)


def finish_kernel(s_ref, far_ref, near0, near1, near2, near3, hidden_hbm, mod_ref, w_own, w1, w2, w3, *refs):
    out_ref, joined_ref, hidden_ref, w0, sems = refs
    nears, ws = [near0, near1, near2, near3], [w0, w1, w2, w3]
    share, items, width_d = hidden_ref.shape
    rows = share * items
    width = w0.shape[0]
    tp = s_ref[6]
    loads = [
        pltpu.make_async_copy(w_own, w0, sems.at[0]),
        pltpu.make_async_copy(
            hidden_hbm.at[pl.ds(pl.multiple_of(tp * share, share), share)], hidden_ref, sems.at[1]
        ),
    ]
    for load in loads:
        load.start()
    ones2 = block_ones(2 * LANES)
    a = lax.broadcasted_iota(jnp.int32, (rows, rows), 0)
    b = lax.broadcasted_iota(jnp.int32, (rows, rows), 1)
    order = ((a % items) * share + a // items == b).astype(F32).astype(BF)
    for g in range(4):
        source = tp ^ g
        mixed = []
        for t in range(width // LANES):
            lanes = slice(t * LANES, (t + 1) * LANES)
            parts = [far_ref[i, source, :, lanes] for i in range(items)]
            parts += [nears[g][i, :, lanes] for i in range(items)]
            sums = spread([x[share:] for x in parts], ones2)
            values = jnp.concatenate([x[:share] for x in parts], axis=0).astype(F32)
            total = values[:rows] * sums[:rows] + values[rows:] * sums[rows:]
            mixed.append((total / (sums[:rows] + sums[rows:])).astype(BF))
        joined_ref[g] = dot(order, jnp.concatenate(mixed, axis=1)).astype(BF)
    for load in loads:
        load.wait()
    gate = mod_ref[2].astype(F32)
    gate = jnp.concatenate([gate, gate], axis=0)[None]
    for n in range(0, width_d, 256):
        lanes = slice(n, min(n + 256, width_d))
        acc = None
        for g in range(4):
            term = dot(joined_ref[g], ws[g][:, lanes]).astype(BF).astype(F32)
            acc = term if acc is None else acc + term
        size = lanes.stop - n
        own = hidden_ref[:, :, lanes].reshape(rows, size).astype(F32).reshape(rows // 8, 8, size)
        new = own + gate[:, :, lanes] * acc.reshape(rows // 8, 8, size)
        out_ref[:, :, lanes] = new.reshape(rows, size).astype(BF).reshape(share, items, size)


def finish(scalars, far, near, hidden, modulation, ws):
    row_total, items, width_d = hidden.shape
    share = row_total // PATCHES
    width = ws[0].shape[0]
    vmem = pl.BlockSpec(memory_space=pltpu.VMEM)
    hbm = pl.BlockSpec(memory_space=pltpu.HBM)
    grid_spec = pltpu.PrefetchScalarGridSpec(
        num_scalar_prefetch=1,
        grid=(1,),
        in_specs=[pl.BlockSpec((items, 4, share + 8, width), lambda s, r: (0, 0, 0, 0))]
        + [vmem] * 4
        + [hbm, pl.BlockSpec((None, 3, items, width_d), lambda s, r: (r[4], 0, 0, 0)), hbm]
        + [vmem] * 3,
        out_specs=pl.BlockSpec((share, items, width_d), lambda s, r: (0, 0, 0)),
        scratch_shapes=[
            pltpu.VMEM((4, share * items, width), BF),
            pltpu.VMEM((share, items, width_d), BF),
            pltpu.VMEM((width, width_d), BF),
            pltpu.SemaphoreType.DMA((2,)),
        ],
    )
    return pl.pallas_call(
        finish_kernel,
        grid_spec=grid_spec,
        out_shape=jax.ShapeDtypeStruct((share, items, width_d), BF),
        compiler_params=params(60),
        cost_estimate=COST,
        name="finish",
    )(scalars, far, *near, hidden, modulation, *ws)


def body(layout, hidden, modulation, w_qkv, w_out, qk_gain, stale_kv, text_kv, text_len):
    slots, tps, groups, w_pairs, core_pairs = layout
    place = lax.axis_index("req")
    tp = lax.axis_index("tp")
    group = place % groups
    patch = place // groups
    items_at = [(patch + o) % PATCHES for o in range(PATCHES)]
    scalars = jnp.stack([v.astype(jnp.int32) for v in items_at + [group, patch, tp]])
    both = ("req", "tp")

    columns = [[g + groups * p for p in range(PATCHES)] for g in range(groups)]
    rings = [[place * tps + t for place in column for t in range(tps)] for column in columns]

    def along_x(value, by):
        return lax.ppermute(value, "req", [(i, (i + by * groups) % slots) for i in range(slots)])

    raws = [lax.dynamic_index_in_dim(stale_kv[0], items_at[o], 1, keepdims=False) for o in range(1, PATCHES)]
    raws, scalars, w_own = lax.optimization_barrier((raws, scalars, w_out))
    kvs = [along_x(raws[o - 1], o) for o in range(1, PATCHES)]
    w_far = lax.ppermute(w_own, both, w_pairs)
    w_near = lax.ppermute(w_own, both, core_pairs)
    mod = jnp.transpose(modulation, (0, 2, 1, 3))
    q, k, v = project(scalars, hidden[0], mod, qk_gain, jnp.transpose(w_qkv, (1, 0, 2)), text_kv[0])
    q_sent, kvs = lax.optimization_barrier((q, kvs))
    q_all = lax.all_to_all(q_sent, "req", 0, 0, axis_index_groups=columns, tiled=True)
    w_across = lax.ppermute(w_far, both, core_pairs)
    owns = own_attention(scalars, q, k, v)
    near = [owns[0]] + [
        lax.ppermute(owns[g], "tp", [(i, i ^ g) for i in range(tps)]) for g in range(1, tps)
    ]
    sent = remote_attention(scalars, jnp.transpose(text_len), q_all, stale_kv[0], kvs)
    sent, near = lax.optimization_barrier((sent, near))
    far = lax.all_to_all(sent, both, 0, 0, axis_index_groups=rings, tiled=True)
    far = far.reshape(PATCHES, tps, *far.shape[1:])
    fresh = jnp.transpose(jnp.stack([k, v], axis=0), (2, 1, 0, 3))
    updated = finish(scalars, far, near, hidden[0], mod, [w_out, w_near, w_far, w_across])
    return (updated[None], fresh[None])


def solution(mesh):
    slots, tps = mesh.shape["req"], mesh.shape["tp"]
    groups = slots // PATCHES
    ring = 8
    w_pairs = []
    for place in range(slots):
        column, high = place // (ring // 2), place % (ring // 2)
        for t in range(tps):
            low, core = t // 2, t % 2
            z = 2 * high + low
            z = (z + (1 if low else -1)) % ring if core else z ^ 1
            target = column * (ring // 2) + z // 2
            w_pairs.append((place * tps + t, target * tps + z % 2 * 2 + core))
    core_pairs = [(i, i ^ 1) for i in range(slots * tps)]
    layout = (slots, tps, groups, w_pairs, core_pairs)
    return jax.shard_map(
        functools.partial(body, layout),
        mesh=mesh,
        in_specs=(
            P("req", None, None, None),
            P(),
            P(None, None, "tp"),
            P("tp", None),
            P(),
            P("req", None, None, None, "tp"),
            P("req", None, None, None, "tp"),
            P(),
        ),
        out_specs=(P("req", "tp", None, None), P("req", None, None, None, "tp")),
        check_vma=False,
    )
```

```python
import functools

import jax
import jax.numpy as jnp
from jax import lax
from jax.experimental import pallas as pl
from jax.experimental.pallas import tpu as pltpu
from jax.sharding import PartitionSpec as P

HEAD = 64
PATCHES = 4
EPSILON = 1e-06
LANES = 128
BF = jnp.bfloat16
F32 = jnp.float32
NT = (((1,), (1,)), ((), ()))
COST = pl.CostEstimate(flops=1000, bytes_accessed=1000, transcendentals=0)


def dot(a, b):
    return jnp.dot(a, b, preferred_element_type=F32)


def params(limit_mb, **kw):
    return pltpu.CompilerParams(vmem_limit_bytes=limit_mb << 20, **kw)


def split_bf(value):
    high = value.astype(BF)
    return high, (value - high.astype(F32)).astype(BF)


def block_ones(rows):
    a = lax.broadcasted_iota(jnp.int32, (rows, LANES), 0) % LANES // HEAD
    b = lax.broadcasted_iota(jnp.int32, (rows, LANES), 1) // HEAD
    return (a == b).astype(F32).astype(BF)


def project_kernel(s_ref, hidden_hbm, mod_ref, gain_ref, w_hbm, text_ref, q_hbm, k_ref, v_ref, *scratch):
    q_ref, hidden_ref, w_ref, xa_ref, xb_ref, scale_ref, shift_ref, y_ref, sems = scratch
    rows = xa_ref.shape[0] // hidden_ref.shape[1]
    blocks = hidden_ref.shape[0] // rows
    items, width_d = hidden_ref.shape[1:]
    loads = [
        pltpu.make_async_copy(
            hidden_hbm.at[pl.ds(b * rows, rows)], hidden_ref.at[pl.ds(b * rows, rows)], sems.at[b]
        )
        for b in range(blocks)
    ]
    columns = w_hbm.shape[2]
    weights = [
        pltpu.make_async_copy(w_hbm.at[j], w_ref.at[:, pl.ds(j * columns, columns)], sems.at[blocks + j])
        for j in range(3)
    ]
    send = pltpu.make_async_copy(q_ref, q_hbm, sems.at[blocks + 3])
    for load in loads[:1] + weights + loads[1:]:
        load.start()
    trows = text_ref.shape[0]
    total = hidden_ref.shape[0]
    for i in range(items):
        for j in range(2):
            q_ref[i, total + j * trows : total + (j + 1) * trows] = text_ref[:, i, j, :]
    width = w_hbm.shape[2]
    tiles = width // LANES
    gain = gain_ref[...]
    gains = jnp.concatenate(
        [gain[0:1] * 0.125] * (width // HEAD) + [gain[1:2]] * (width // HEAD), axis=1
    )
    shift = mod_ref[0].astype(F32)
    scale = 1.0 + mod_ref[1].astype(F32)
    shift_ref[...] = jnp.concatenate([shift, shift], axis=0)
    scale_ref[...] = jnp.concatenate([scale, scale], axis=0)
    wide = 2 * LANES
    r = lax.broadcasted_iota(jnp.int32, (2 * wide, wide), 0) % wide // HEAD
    c = lax.broadcasted_iota(jnp.int32, (2 * wide, wide), 1) // HEAD
    ones = (r == c).astype(F32).astype(BF)

    def norm_rows(block, x_ref, c):
        first = block * rows + c * 4
        x = hidden_ref[first : first + 4].reshape(16, width_d).astype(F32).reshape(2, 8, width_d)
        center = x - jnp.mean(x, axis=-1, keepdims=True)
        variance = jnp.mean(center * center, axis=-1, keepdims=True)
        normed = center * lax.rsqrt(variance + EPSILON)
        out = normed * scale_ref[...][None] + shift_ref[...][None]
        x_ref[c * 16 : c * 16 + 16, :] = out.reshape(16, width_d).astype(BF)

    def finish_tile(block, n, y):
        if n + wide <= 2 * width:
            high, low = split_bf(y * y)
            square = dot(jnp.concatenate([high, low], axis=1), ones) * (1.0 / HEAD)
            y = y * lax.rsqrt(square + EPSILON) * gains[:, n : n + wide]
        for t in range(y.shape[1] // LANES):
            tile = n // LANES + t
            j = tile // tiles
            y_ref[tile] = y[:, t * LANES : (t + 1) * LANES]
            where = slice(block * rows, (block + 1) * rows)
            to = slice(tile % tiles * LANES, (tile % tiles + 1) * LANES)
            for i in range(items):
                (q_ref, k_ref, v_ref)[j][i, where, to] = y_ref[tile, pl.ds(i, rows, stride=items), :].astype(BF)

    chunks = rows // 4
    pending = []
    for block in range(blocks + 1):
        now, later = (xb_ref, xa_ref) if block % 2 == 0 else (xa_ref, xb_ref)
        if block < blocks:
            loads[block].wait()
        if block == 0:
            for c in range(chunks):
                norm_rows(0, later, c)
            for load in weights:
                load.wait()
            continue
        starts = list(range(0, 3 * width, wide))
        for at, n in enumerate(starts):
            y = dot(now[...], w_ref[:, n : min(n + wide, 3 * width)])
            if block < blocks:
                for c in range(at * chunks // len(starts), (at + 1) * chunks // len(starts)):
                    norm_rows(block, later, c)
            if pending:
                done = pending.pop()
                finish_tile(*done)
                if done[0] == blocks - 1 and done[1] < width <= done[1] + wide:
                    send.start()
            pending.append((block - 1, n, y))
    finish_tile(*pending.pop())
    send.wait()


def project(scalars, hidden, modulation, gains, w, text):
    row_total, items, width_d = hidden.shape
    width = w.shape[2]
    rows = 128
    q_rows = row_total + 2 * text.shape[0]
    vmem = pl.BlockSpec(memory_space=pltpu.VMEM)
    grid_spec = pltpu.PrefetchScalarGridSpec(
        num_scalar_prefetch=1,
        grid=(1,),
        in_specs=[
            pl.BlockSpec(memory_space=pltpu.HBM),
            pl.BlockSpec((None, 3, items, width_d), lambda s, r: (r[4], 0, 0, 0)),
            vmem,
            pl.BlockSpec(memory_space=pltpu.HBM),
            vmem,
        ],
        out_specs=[pl.BlockSpec(memory_space=pltpu.HBM)] + [vmem] * 2,
        scratch_shapes=[
            pltpu.VMEM((items, q_rows, width), BF),
            pltpu.VMEM((row_total, items, width_d), BF),
            pltpu.VMEM((width_d, 3 * width), BF),
            pltpu.VMEM((rows * items, width_d), BF),
            pltpu.VMEM((rows * items, width_d), BF),
            pltpu.VMEM((8, width_d), F32),
            pltpu.VMEM((8, width_d), F32),
            pltpu.VMEM((3 * width // LANES, rows * items, LANES), F32),
            pltpu.SemaphoreType.DMA((row_total // rows + 4,)),
        ],
    )
    return pl.pallas_call(
        project_kernel,
        grid_spec=grid_spec,
        out_shape=[jax.ShapeDtypeStruct((items, q_rows, width), BF)]
        + [jax.ShapeDtypeStruct((items, row_total, width), BF)] * 2,
        compiler_params=params(60),
        cost_estimate=COST,
        name="project",
    )(scalars, hidden, modulation, gains, w, text)


def half_masks():
    lane = lax.broadcasted_iota(jnp.int32, (8, LANES), 1)
    return [(lane < HEAD).astype(F32)[0:1].astype(BF), (lane >= HEAD).astype(F32)[0:1].astype(BF)]


def weigh(values, mask, valid=None):
    ones = jnp.broadcast_to(mask, values.shape)
    both = jnp.concatenate([values * mask, ones], axis=1)
    return both if valid is None else both * valid


def sums_tiles(sums, share):
    count = sums.shape[0] // share
    r = lax.broadcasted_iota(jnp.int32, (share, LANES), 0)
    c = lax.broadcasted_iota(jnp.int32, (share, LANES), 1) % HEAD
    own = (r == c).astype(F32)
    at = lax.broadcasted_iota(jnp.int32, (8, LANES), 0)
    tiles = []
    for u in range(count):
        line = jnp.sum(sums[u * share : (u + 1) * share] * own, axis=0, keepdims=True)
        high = line.astype(BF).astype(F32)
        tiles.append(jnp.where(at == 0, high, jnp.where(at == 1, line - high, 0.0)).astype(BF))
    return tiles


def own_kernel(s_ref, q_ref, k_ref, v_ref, *refs):
    out_refs, part_ref, sems = refs[:PATCHES], refs[PATCHES], refs[PATCHES + 1]
    items, rows, width = k_ref.shape
    share = rows // PATCHES
    masks = half_masks()
    for i in range(items):
        for t in range(width // LANES):
            lanes = slice(t * LANES, (t + 1) * LANES)
            kp, vp, qp = k_ref[i, :, lanes], v_ref[i, :, lanes], q_ref[i, 0:rows, lanes]
            ps = [
                jnp.exp(lax.dot_general(qp * mask, kp, NT, preferred_element_type=F32)).astype(BF)
                for mask in masks
            ]
            acc = dot(
                jnp.concatenate(ps, axis=1), jnp.concatenate([weigh(vp, mask) for mask in masks], axis=0)
            )
            sums = acc[:, LANES:]
            part = (acc[:, :LANES] / sums).astype(BF)
            for u, tile in enumerate(sums_tiles(sums, share)):
                part_ref[u, i, 0:share, lanes] = part[u * share : (u + 1) * share]
                part_ref[u, i, share : share + 8, lanes] = tile
    copies = [
        pltpu.make_async_copy(part_ref.at[s_ref[6] ^ g], out_refs[g], sems.at[g]) for g in range(PATCHES)
    ]
    for copy in copies:
        copy.start()
    for copy in copies:
        copy.wait()


def own_attention(scalars, q, k, v):
    items, rows, width = k.shape
    share = rows // PATCHES
    vmem = pl.BlockSpec(memory_space=pltpu.VMEM)
    return pl.pallas_call(
        own_kernel,
        in_specs=[pl.BlockSpec(memory_space=pltpu.SMEM)] + [vmem] * 3,
        out_specs=[pl.BlockSpec(memory_space=pltpu.HBM)] * PATCHES,
        out_shape=[jax.ShapeDtypeStruct((items, share + 8, width), BF)] * PATCHES,
        scratch_shapes=[
            pltpu.VMEM((PATCHES, items, share + 8, width), BF),
            pltpu.SemaphoreType.DMA((PATCHES,)),
        ],
        compiler_params=params(60),
        cost_estimate=COST,
        name="own",
    )(scalars, q, k, v)


def remote_kernel(s_ref, length_ref, *refs):
    q_all, kv_refs = refs[0], refs[1 : 1 + PATCHES]
    out_ref, text_ref = refs[1 + PATCHES :]
    rows = kv_refs[0].shape[0]
    trows = (q_all.shape[1] - rows) // 2
    share = rows // PATCHES
    group, patch = s_ref[4], s_ref[5]
    q_refs = [q_all.at[lax.rem(patch - o + PATCHES, PATCHES)] for o in range(PATCHES)]
    length = length_ref[patch, group]
    masks = half_masks()
    text_ref[...] = jnp.zeros_like(text_ref)
    good = lax.broadcasted_iota(jnp.int32, (rows, 2 * LANES), 0) < length
    for p in range(PATCHES):
        for j in range(2):
            first = rows + j * trows
            text_ref[j, p * trows : (p + 1) * trows] = q_all[p, first : first + trows].astype(F32)
    valid = good.astype(F32).astype(BF)
    text_k, text_v = text_ref[0].astype(BF), text_ref[1].astype(BF)
    accs = [None] * PATCHES
    for c in range(PATCHES + 1):
        if c == PATCHES:
            keys, values = text_k, [weigh(text_v, mask, valid) for mask in masks]
        else:
            pair = kv_refs[c]
            keys, values = pair[:, 0, :], pair[:, 1, :]
            values = [weigh(values, mask) for mask in masks]
        which = [o for o in range(PATCHES) if o != c]
        queries = jnp.concatenate([q_refs[o][0:rows] for o in which], axis=0)
        ps = [
            jnp.exp(lax.dot_general(queries * mask, keys, NT, preferred_element_type=F32)).astype(BF)
            for mask in masks
        ]
        term = dot(jnp.concatenate(ps, axis=1), jnp.concatenate(values, axis=0))
        for at, o in enumerate(which):
            piece = term[at * rows : (at + 1) * rows]
            accs[o] = piece if accs[o] is None else accs[o] + piece
    for o in range(PATCHES):
        sums = accs[o][:, LANES:]
        part = (accs[o][:, :LANES] / sums).astype(BF)
        base = lax.rem(patch - o + PATCHES, PATCHES) * PATCHES
        for u, tile in enumerate(sums_tiles(sums, share)):
            out_ref[base + u, 0:share] = part[u * share : (u + 1) * share]
            out_ref[base + u, share : share + 8] = tile


def remote_attention(scalars, lengths, q, stale, kvs):
    rows, _, _, width = stale.shape
    q_rows = q.shape[1]
    share = rows // PATCHES
    grid_spec = pltpu.PrefetchScalarGridSpec(
        num_scalar_prefetch=2,
        grid=(width // LANES,),
        in_specs=[pl.BlockSpec((PATCHES, q_rows, LANES), lambda s, r, t: (0, 0, s))]
        + [pl.BlockSpec((rows, None, 2, LANES), lambda s, r, t: (0, r[0], 0, s))]
        + [pl.BlockSpec((rows, 2, LANES), lambda s, r, t: (0, 0, s))] * (PATCHES - 1),
        out_specs=pl.BlockSpec((PATCHES * PATCHES, share + 8, LANES), lambda s, r, t: (0, 0, s)),
        scratch_shapes=[pltpu.VMEM((2, rows, LANES), F32)],
    )
    return pl.pallas_call(
        remote_kernel,
        grid_spec=grid_spec,
        out_shape=jax.ShapeDtypeStruct((PATCHES * PATCHES, share + 8, width), BF),
        compiler_params=params(63),
        cost_estimate=COST,
        name="remote",
    )(scalars, lengths, q, stale, *kvs)


def spread(lines, ones2):
    r = lax.broadcasted_iota(jnp.int32, (HEAD, LANES), 0)
    c = lax.broadcasted_iota(jnp.int32, (HEAD, LANES), 1) % HEAD
    parts = []
    for line in lines:
        f = line.astype(F32)
        parts.append(
            jnp.concatenate(
                [jnp.where(r == c, f[0:1], 0.0), jnp.where(r == c, f[1:2], 0.0)], axis=1
            ).astype(BF)
        )
    return dot(jnp.concatenate(parts, axis=0), ones2)


def finish_kernel(s_ref, far_ref, near0, near1, near2, near3, hidden_hbm, mod_ref, w_own, w1, w2, w3, *refs):
    out_ref, joined_ref, hidden_ref, w0, sems = refs
    nears, ws = [near0, near1, near2, near3], [w0, w1, w2, w3]
    share, items, width_d = hidden_ref.shape
    rows = share * items
    width = w0.shape[0]
    tp = s_ref[6]
    loads = [
        pltpu.make_async_copy(w_own, w0, sems.at[0]),
        pltpu.make_async_copy(
            hidden_hbm.at[pl.ds(pl.multiple_of(tp * share, share), share)], hidden_ref, sems.at[1]
        ),
    ]
    for load in loads:
        load.start()
    ones2 = block_ones(2 * LANES)
    a = lax.broadcasted_iota(jnp.int32, (rows, rows), 0)
    b = lax.broadcasted_iota(jnp.int32, (rows, rows), 1)
    order = ((a % items) * share + a // items == b).astype(F32).astype(BF)
    for g in range(4):
        source = tp ^ g
        mixed = []
        for t in range(width // LANES):
            lanes = slice(t * LANES, (t + 1) * LANES)
            parts = [far_ref[i, source, :, lanes] for i in range(items)]
            parts += [nears[g][i, :, lanes] for i in range(items)]
            sums = spread([x[share:] for x in parts], ones2)
            values = jnp.concatenate([x[:share] for x in parts], axis=0).astype(F32)
            total = values[:rows] * sums[:rows] + values[rows:] * sums[rows:]
            mixed.append((total / (sums[:rows] + sums[rows:])).astype(BF))
        joined_ref[g] = dot(order, jnp.concatenate(mixed, axis=1)).astype(BF)
    for load in loads:
        load.wait()
    gate = mod_ref[2].astype(F32)
    gate = jnp.concatenate([gate, gate], axis=0)[None]
    for n in range(0, width_d, 256):
        lanes = slice(n, min(n + 256, width_d))
        acc = None
        for g in range(4):
            term = dot(joined_ref[g], ws[g][:, lanes]).astype(BF).astype(F32)
            acc = term if acc is None else acc + term
        size = lanes.stop - n
        own = hidden_ref[:, :, lanes].reshape(rows, size).astype(F32).reshape(rows // 8, 8, size)
        new = own + gate[:, :, lanes] * acc.reshape(rows // 8, 8, size)
        out_ref[:, :, lanes] = new.reshape(rows, size).astype(BF).reshape(share, items, size)


def finish(scalars, far, near, hidden, modulation, ws):
    row_total, items, width_d = hidden.shape
    share = row_total // PATCHES
    width = ws[0].shape[0]
    vmem = pl.BlockSpec(memory_space=pltpu.VMEM)
    hbm = pl.BlockSpec(memory_space=pltpu.HBM)
    grid_spec = pltpu.PrefetchScalarGridSpec(
        num_scalar_prefetch=1,
        grid=(1,),
        in_specs=[pl.BlockSpec((items, 4, share + 8, width), lambda s, r: (0, 0, 0, 0))]
        + [vmem] * 4
        + [hbm, pl.BlockSpec((None, 3, items, width_d), lambda s, r: (r[4], 0, 0, 0)), hbm]
        + [vmem] * 3,
        out_specs=pl.BlockSpec((share, items, width_d), lambda s, r: (0, 0, 0)),
        scratch_shapes=[
            pltpu.VMEM((4, share * items, width), BF),
            pltpu.VMEM((share, items, width_d), BF),
            pltpu.VMEM((width, width_d), BF),
            pltpu.SemaphoreType.DMA((2,)),
        ],
    )
    return pl.pallas_call(
        finish_kernel,
        grid_spec=grid_spec,
        out_shape=jax.ShapeDtypeStruct((share, items, width_d), BF),
        compiler_params=params(60),
        cost_estimate=COST,
        name="finish",
    )(scalars, far, *near, hidden, modulation, *ws)


def body(layout, hidden, modulation, w_qkv, w_out, qk_gain, stale_kv, text_kv, text_len):
    slots, tps, groups, w_pairs, core_pairs = layout
    place = lax.axis_index("req")
    tp = lax.axis_index("tp")
    group = place % groups
    patch = place // groups
    items_at = [(patch + o) % PATCHES for o in range(PATCHES)]
    scalars = jnp.stack([v.astype(jnp.int32) for v in items_at + [group, patch, tp]])
    both = ("req", "tp")

    columns = [[g + groups * p for p in range(PATCHES)] for g in range(groups)]
    rings = [[place * tps + t for place in column for t in range(tps)] for column in columns]

    def along_x(value, by):
        return lax.ppermute(value, "req", [(i, (i + by * groups) % slots) for i in range(slots)])

    raws = [lax.dynamic_index_in_dim(stale_kv[0], items_at[o], 1, keepdims=False) for o in range(1, PATCHES)]
    raws, scalars, w_own = lax.optimization_barrier((raws, scalars, w_out))
    kvs = [along_x(raws[o - 1], o) for o in range(1, PATCHES)]
    w_far = lax.ppermute(w_own, both, w_pairs)
    w_near = lax.ppermute(w_own, both, core_pairs)
    mod = jnp.transpose(modulation, (0, 2, 1, 3))
    q, k, v = project(scalars, hidden[0], mod, qk_gain, jnp.transpose(w_qkv, (1, 0, 2)), text_kv[0])
    q_sent, kvs = lax.optimization_barrier((q, kvs))
    q_all = lax.all_to_all(q_sent, "req", 0, 0, axis_index_groups=columns, tiled=True)
    w_across = lax.ppermute(w_far, both, core_pairs)
    owns = own_attention(scalars, q, k, v)
    near = [owns[0]] + [
        lax.ppermute(owns[g], "tp", [(i, i ^ g) for i in range(tps)]) for g in range(1, tps)
    ]
    sent = remote_attention(scalars, jnp.transpose(text_len), q_all, stale_kv[0], kvs)
    sent, near = lax.optimization_barrier((sent, near))
    far = lax.all_to_all(sent, both, 0, 0, axis_index_groups=rings, tiled=True)
    far = far.reshape(PATCHES, tps, *far.shape[1:])
    fresh = jnp.transpose(jnp.stack([k, v], axis=0), (2, 1, 0, 3))
    updated = finish(scalars, far, near, hidden[0], mod, [w_out, w_near, w_far, w_across])
    return (updated[None], fresh[None])


def solution(mesh):
    slots, tps = mesh.shape["req"], mesh.shape["tp"]
    groups = slots // PATCHES
    ring = 8
    w_pairs = []
    for place in range(slots):
        column, high = place // (ring // 2), place % (ring // 2)
        for t in range(tps):
            low, core = t // 2, t % 2
            z = 2 * high + low
            z = (z + (1 if low else -1)) % ring if core else z ^ 1
            target = column * (ring // 2) + z // 2
            w_pairs.append((place * tps + t, target * tps + z % 2 * 2 + core))
    core_pairs = [(i, i ^ 1) for i in range(slots * tps)]
    layout = (slots, tps, groups, w_pairs, core_pairs)
    return jax.shard_map(
        functools.partial(body, layout),
        mesh=mesh,
        in_specs=(
            P("req", None, None, None),
            P(),
            P(None, None, "tp"),
            P("tp", None),
            P(),
            P("req", None, None, None, "tp"),
            P("req", None, None, None, "tp"),
            P(),
        ),
        out_specs=(P("req", "tp", None, None), P("req", None, None, None, "tp")),
        check_vma=False,
    )
```

```python
import functools

import jax
import jax.numpy as jnp
from jax import lax
from jax.experimental import pallas as pl
from jax.experimental.pallas import tpu as pltpu
from jax.sharding import PartitionSpec as P

HEAD = 64
PATCHES = 4
EPSILON = 1e-06
LANES = 128
BF = jnp.bfloat16
F32 = jnp.float32
NT = (((1,), (1,)), ((), ()))
COST = pl.CostEstimate(flops=1000, bytes_accessed=1000, transcendentals=0)


def dot(a, b):
    return jnp.dot(a, b, preferred_element_type=F32)


def params(limit_mb, **kw):
    return pltpu.CompilerParams(vmem_limit_bytes=limit_mb << 20, **kw)


def split_bf(value):
    high = value.astype(BF)
    return high, (value - high.astype(F32)).astype(BF)


def block_ones(rows):
    a = lax.broadcasted_iota(jnp.int32, (rows, LANES), 0) % LANES // HEAD
    b = lax.broadcasted_iota(jnp.int32, (rows, LANES), 1) // HEAD
    return (a == b).astype(F32).astype(BF)


def project_kernel(s_ref, hidden_hbm, mod_ref, gain_ref, w_hbm, text_ref, q_hbm, k_ref, v_ref, *scratch):
    q_ref, hidden_ref, w_ref, xa_ref, xb_ref, scale_ref, shift_ref, y_ref, sems = scratch
    rows = xa_ref.shape[0] // hidden_ref.shape[1]
    blocks = hidden_ref.shape[0] // rows
    items, width_d = hidden_ref.shape[1:]
    loads = [
        pltpu.make_async_copy(
            hidden_hbm.at[pl.ds(b * rows, rows)], hidden_ref.at[pl.ds(b * rows, rows)], sems.at[b]
        )
        for b in range(blocks)
    ]
    columns = w_hbm.shape[2]
    weights = [
        pltpu.make_async_copy(w_hbm.at[j], w_ref.at[:, pl.ds(j * columns, columns)], sems.at[blocks + j])
        for j in range(3)
    ]
    send = pltpu.make_async_copy(q_ref, q_hbm, sems.at[blocks + 3])
    for load in loads[:1] + weights + loads[1:]:
        load.start()
    trows = text_ref.shape[0]
    total = hidden_ref.shape[0]
    for i in range(items):
        for j in range(2):
            q_ref[i, total + j * trows : total + (j + 1) * trows] = text_ref[:, i, j, :]
    width = w_hbm.shape[2]
    tiles = width // LANES
    gain = gain_ref[...]
    gains = jnp.concatenate(
        [gain[0:1] * 0.125] * (width // HEAD) + [gain[1:2]] * (width // HEAD), axis=1
    )
    shift = mod_ref[0].astype(F32)
    scale = 1.0 + mod_ref[1].astype(F32)
    shift_ref[...] = jnp.concatenate([shift, shift], axis=0)
    scale_ref[...] = jnp.concatenate([scale, scale], axis=0)
    wide = 2 * LANES
    r = lax.broadcasted_iota(jnp.int32, (2 * wide, wide), 0) % wide // HEAD
    c = lax.broadcasted_iota(jnp.int32, (2 * wide, wide), 1) // HEAD
    ones = (r == c).astype(F32).astype(BF)

    def norm_rows(block, x_ref, c):
        first = block * rows + c * 4
        x = hidden_ref[first : first + 4].reshape(16, width_d).astype(F32).reshape(2, 8, width_d)
        center = x - jnp.mean(x, axis=-1, keepdims=True)
        variance = jnp.mean(center * center, axis=-1, keepdims=True)
        normed = center * lax.rsqrt(variance + EPSILON)
        out = normed * scale_ref[...][None] + shift_ref[...][None]
        x_ref[c * 16 : c * 16 + 16, :] = out.reshape(16, width_d).astype(BF)

    def finish_tile(block, n, y):
        if n + wide <= 2 * width:
            high, low = split_bf(y * y)
            square = dot(jnp.concatenate([high, low], axis=1), ones) * (1.0 / HEAD)
            y = y * lax.rsqrt(square + EPSILON) * gains[:, n : n + wide]
        for t in range(y.shape[1] // LANES):
            tile = n // LANES + t
            j = tile // tiles
            y_ref[tile] = y[:, t * LANES : (t + 1) * LANES]
            where = slice(block * rows, (block + 1) * rows)
            to = slice(tile % tiles * LANES, (tile % tiles + 1) * LANES)
            for i in range(items):
                (q_ref, k_ref, v_ref)[j][i, where, to] = y_ref[tile, pl.ds(i, rows, stride=items), :].astype(BF)

    chunks = rows // 4
    pending = []
    for block in range(blocks + 1):
        now, later = (xb_ref, xa_ref) if block % 2 == 0 else (xa_ref, xb_ref)
        if block < blocks:
            loads[block].wait()
        if block == 0:
            for c in range(chunks):
                norm_rows(0, later, c)
            for load in weights:
                load.wait()
            continue
        starts = list(range(0, 3 * width, wide))
        for at, n in enumerate(starts):
            y = dot(now[...], w_ref[:, n : min(n + wide, 3 * width)])
            if block < blocks:
                for c in range(at * chunks // len(starts), (at + 1) * chunks // len(starts)):
                    norm_rows(block, later, c)
            if pending:
                done = pending.pop()
                finish_tile(*done)
                if done[0] == blocks - 1 and done[1] < width <= done[1] + wide:
                    send.start()
            pending.append((block - 1, n, y))
    finish_tile(*pending.pop())
    send.wait()


def project(scalars, hidden, modulation, gains, w, text):
    row_total, items, width_d = hidden.shape
    width = w.shape[2]
    rows = 128
    q_rows = row_total + 2 * text.shape[0]
    vmem = pl.BlockSpec(memory_space=pltpu.VMEM)
    grid_spec = pltpu.PrefetchScalarGridSpec(
        num_scalar_prefetch=1,
        grid=(1,),
        in_specs=[
            pl.BlockSpec(memory_space=pltpu.HBM),
            pl.BlockSpec((None, 3, items, width_d), lambda s, r: (r[4], 0, 0, 0)),
            vmem,
            pl.BlockSpec(memory_space=pltpu.HBM),
            vmem,
        ],
        out_specs=[pl.BlockSpec(memory_space=pltpu.HBM)] + [vmem] * 2,
        scratch_shapes=[
            pltpu.VMEM((items, q_rows, width), BF),
            pltpu.VMEM((row_total, items, width_d), BF),
            pltpu.VMEM((width_d, 3 * width), BF),
            pltpu.VMEM((rows * items, width_d), BF),
            pltpu.VMEM((rows * items, width_d), BF),
            pltpu.VMEM((8, width_d), F32),
            pltpu.VMEM((8, width_d), F32),
            pltpu.VMEM((3 * width // LANES, rows * items, LANES), F32),
            pltpu.SemaphoreType.DMA((row_total // rows + 4,)),
        ],
    )
    return pl.pallas_call(
        project_kernel,
        grid_spec=grid_spec,
        out_shape=[jax.ShapeDtypeStruct((items, q_rows, width), BF)]
        + [jax.ShapeDtypeStruct((items, row_total, width), BF)] * 2,
        compiler_params=params(60),
        cost_estimate=COST,
        name="project",
    )(scalars, hidden, modulation, gains, w, text)


def half_masks():
    lane = lax.broadcasted_iota(jnp.int32, (8, LANES), 1)
    return [(lane < HEAD).astype(F32)[0:1].astype(BF), (lane >= HEAD).astype(F32)[0:1].astype(BF)]


def weigh(values, mask, valid=None):
    ones = jnp.broadcast_to(mask, values.shape)
    both = jnp.concatenate([values * mask, ones], axis=1)
    return both if valid is None else both * valid


def sums_tiles(sums, share):
    count = sums.shape[0] // share
    r = lax.broadcasted_iota(jnp.int32, (share, LANES), 0)
    c = lax.broadcasted_iota(jnp.int32, (share, LANES), 1) % HEAD
    own = (r == c).astype(F32)
    at = lax.broadcasted_iota(jnp.int32, (8, LANES), 0)
    tiles = []
    for u in range(count):
        line = jnp.sum(sums[u * share : (u + 1) * share] * own, axis=0, keepdims=True)
        high = line.astype(BF).astype(F32)
        tiles.append(jnp.where(at == 0, high, jnp.where(at == 1, line - high, 0.0)).astype(BF))
    return tiles


def own_kernel(s_ref, q_ref, k_ref, v_ref, *refs):
    out_refs, part_ref, sems = refs[:PATCHES], refs[PATCHES], refs[PATCHES + 1]
    items, rows, width = k_ref.shape
    share = rows // PATCHES
    masks = half_masks()
    for i in range(items):
        for t in range(width // LANES):
            lanes = slice(t * LANES, (t + 1) * LANES)
            kp, vp, qp = k_ref[i, :, lanes], v_ref[i, :, lanes], q_ref[i, 0:rows, lanes]
            ps = [
                jnp.exp(lax.dot_general(qp * mask, kp, NT, preferred_element_type=F32)).astype(BF)
                for mask in masks
            ]
            acc = dot(
                jnp.concatenate(ps, axis=1), jnp.concatenate([weigh(vp, mask) for mask in masks], axis=0)
            )
            sums = acc[:, LANES:]
            part = (acc[:, :LANES] / sums).astype(BF)
            for u, tile in enumerate(sums_tiles(sums, share)):
                part_ref[u, i, 0:share, lanes] = part[u * share : (u + 1) * share]
                part_ref[u, i, share : share + 8, lanes] = tile
    copies = [
        pltpu.make_async_copy(part_ref.at[s_ref[6] ^ g], out_refs[g], sems.at[g]) for g in range(PATCHES)
    ]
    for copy in copies:
        copy.start()
    for copy in copies:
        copy.wait()


def own_attention(scalars, q, k, v):
    items, rows, width = k.shape
    share = rows // PATCHES
    vmem = pl.BlockSpec(memory_space=pltpu.VMEM)
    return pl.pallas_call(
        own_kernel,
        in_specs=[pl.BlockSpec(memory_space=pltpu.SMEM)] + [vmem] * 3,
        out_specs=[pl.BlockSpec(memory_space=pltpu.HBM)] * PATCHES,
        out_shape=[jax.ShapeDtypeStruct((items, share + 8, width), BF)] * PATCHES,
        scratch_shapes=[
            pltpu.VMEM((PATCHES, items, share + 8, width), BF),
            pltpu.SemaphoreType.DMA((PATCHES,)),
        ],
        compiler_params=params(60),
        cost_estimate=COST,
        name="own",
    )(scalars, q, k, v)


def remote_kernel(s_ref, length_ref, *refs):
    q_all, kv_refs = refs[0], refs[1 : 1 + PATCHES]
    out_ref, text_ref = refs[1 + PATCHES :]
    rows = kv_refs[0].shape[0]
    trows = (q_all.shape[1] - rows) // 2
    share = rows // PATCHES
    group, patch = s_ref[4], s_ref[5]
    q_refs = [q_all.at[lax.rem(patch - o + PATCHES, PATCHES)] for o in range(PATCHES)]
    length = length_ref[patch, group]
    masks = half_masks()
    text_ref[...] = jnp.zeros_like(text_ref)
    good = lax.broadcasted_iota(jnp.int32, (rows, 2 * LANES), 0) < length
    for p in range(PATCHES):
        for j in range(2):
            first = rows + j * trows
            text_ref[j, p * trows : (p + 1) * trows] = q_all[p, first : first + trows].astype(F32)
    valid = good.astype(F32).astype(BF)
    text_k, text_v = text_ref[0].astype(BF), text_ref[1].astype(BF)
    accs = [None] * PATCHES
    for c in range(PATCHES + 1):
        if c == PATCHES:
            keys, values = text_k, [weigh(text_v, mask, valid) for mask in masks]
        else:
            pair = kv_refs[c]
            keys, values = pair[:, 0, :], pair[:, 1, :]
            values = [weigh(values, mask) for mask in masks]
        which = [o for o in range(PATCHES) if o != c]
        queries = jnp.concatenate([q_refs[o][0:rows] for o in which], axis=0)
        ps = [
            jnp.exp(lax.dot_general(queries * mask, keys, NT, preferred_element_type=F32)).astype(BF)
            for mask in masks
        ]
        term = dot(jnp.concatenate(ps, axis=1), jnp.concatenate(values, axis=0))
        for at, o in enumerate(which):
            piece = term[at * rows : (at + 1) * rows]
            accs[o] = piece if accs[o] is None else accs[o] + piece
    for o in range(PATCHES):
        sums = accs[o][:, LANES:]
        part = (accs[o][:, :LANES] / sums).astype(BF)
        base = lax.rem(patch - o + PATCHES, PATCHES) * PATCHES
        for u, tile in enumerate(sums_tiles(sums, share)):
            out_ref[base + u, 0:share] = part[u * share : (u + 1) * share]
            out_ref[base + u, share : share + 8] = tile


def remote_attention(scalars, lengths, q, stale, kvs):
    rows, _, _, width = stale.shape
    q_rows = q.shape[1]
    share = rows // PATCHES
    grid_spec = pltpu.PrefetchScalarGridSpec(
        num_scalar_prefetch=2,
        grid=(width // LANES,),
        in_specs=[pl.BlockSpec((PATCHES, q_rows, LANES), lambda s, r, t: (0, 0, s))]
        + [pl.BlockSpec((rows, None, 2, LANES), lambda s, r, t: (0, r[0], 0, s))]
        + [pl.BlockSpec((rows, 2, LANES), lambda s, r, t: (0, 0, s))] * (PATCHES - 1),
        out_specs=pl.BlockSpec((PATCHES * PATCHES, share + 8, LANES), lambda s, r, t: (0, 0, s)),
        scratch_shapes=[pltpu.VMEM((2, rows, LANES), F32)],
    )
    return pl.pallas_call(
        remote_kernel,
        grid_spec=grid_spec,
        out_shape=jax.ShapeDtypeStruct((PATCHES * PATCHES, share + 8, width), BF),
        compiler_params=params(63),
        cost_estimate=COST,
        name="remote",
    )(scalars, lengths, q, stale, *kvs)


def spread(lines, ones2):
    r = lax.broadcasted_iota(jnp.int32, (HEAD, LANES), 0)
    c = lax.broadcasted_iota(jnp.int32, (HEAD, LANES), 1) % HEAD
    parts = []
    for line in lines:
        f = line.astype(F32)
        parts.append(
            jnp.concatenate(
                [jnp.where(r == c, f[0:1], 0.0), jnp.where(r == c, f[1:2], 0.0)], axis=1
            ).astype(BF)
        )
    return dot(jnp.concatenate(parts, axis=0), ones2)


def finish_kernel(s_ref, far_ref, near0, near1, near2, near3, hidden_hbm, mod_ref, w_own, w1, w2, w3, *refs):
    out_ref, joined_ref, hidden_ref, w0, sems = refs
    nears, ws = [near0, near1, near2, near3], [w0, w1, w2, w3]
    share, items, width_d = hidden_ref.shape
    rows = share * items
    width = w0.shape[0]
    tp = s_ref[6]
    loads = [
        pltpu.make_async_copy(w_own, w0, sems.at[0]),
        pltpu.make_async_copy(
            hidden_hbm.at[pl.ds(pl.multiple_of(tp * share, share), share)], hidden_ref, sems.at[1]
        ),
    ]
    for load in loads:
        load.start()
    ones2 = block_ones(2 * LANES)
    a = lax.broadcasted_iota(jnp.int32, (rows, rows), 0)
    b = lax.broadcasted_iota(jnp.int32, (rows, rows), 1)
    order = ((a % items) * share + a // items == b).astype(F32).astype(BF)
    for g in range(4):
        source = tp ^ g
        mixed = []
        for t in range(width // LANES):
            lanes = slice(t * LANES, (t + 1) * LANES)
            parts = [far_ref[i, source, :, lanes] for i in range(items)]
            parts += [nears[g][i, :, lanes] for i in range(items)]
            sums = spread([x[share:] for x in parts], ones2)
            values = jnp.concatenate([x[:share] for x in parts], axis=0).astype(F32)
            total = values[:rows] * sums[:rows] + values[rows:] * sums[rows:]
            mixed.append((total / (sums[:rows] + sums[rows:])).astype(BF))
        joined_ref[g] = dot(order, jnp.concatenate(mixed, axis=1)).astype(BF)
    for load in loads:
        load.wait()
    gate = mod_ref[2].astype(F32)
    gate = jnp.concatenate([gate, gate], axis=0)[None]
    for n in range(0, width_d, 256):
        lanes = slice(n, min(n + 256, width_d))
        acc = None
        for g in range(4):
            term = dot(joined_ref[g], ws[g][:, lanes]).astype(BF).astype(F32)
            acc = term if acc is None else acc + term
        size = lanes.stop - n
        own = hidden_ref[:, :, lanes].reshape(rows, size).astype(F32).reshape(rows // 8, 8, size)
        new = own + gate[:, :, lanes] * acc.reshape(rows // 8, 8, size)
        out_ref[:, :, lanes] = new.reshape(rows, size).astype(BF).reshape(share, items, size)


def finish(scalars, far, near, hidden, modulation, ws):
    row_total, items, width_d = hidden.shape
    share = row_total // PATCHES
    width = ws[0].shape[0]
    vmem = pl.BlockSpec(memory_space=pltpu.VMEM)
    hbm = pl.BlockSpec(memory_space=pltpu.HBM)
    grid_spec = pltpu.PrefetchScalarGridSpec(
        num_scalar_prefetch=1,
        grid=(1,),
        in_specs=[pl.BlockSpec((items, 4, share + 8, width), lambda s, r: (0, 0, 0, 0))]
        + [vmem] * 4
        + [hbm, pl.BlockSpec((None, 3, items, width_d), lambda s, r: (r[4], 0, 0, 0)), hbm]
        + [vmem] * 3,
        out_specs=pl.BlockSpec((share, items, width_d), lambda s, r: (0, 0, 0)),
        scratch_shapes=[
            pltpu.VMEM((4, share * items, width), BF),
            pltpu.VMEM((share, items, width_d), BF),
            pltpu.VMEM((width, width_d), BF),
            pltpu.SemaphoreType.DMA((2,)),
        ],
    )
    return pl.pallas_call(
        finish_kernel,
        grid_spec=grid_spec,
        out_shape=jax.ShapeDtypeStruct((share, items, width_d), BF),
        compiler_params=params(54),
        cost_estimate=COST,
        name="finish",
    )(scalars, far, *near, hidden, modulation, *ws)


def body(layout, hidden, modulation, w_qkv, w_out, qk_gain, stale_kv, text_kv, text_len):
    slots, tps, groups, w_pairs, core_pairs = layout
    place = lax.axis_index("req")
    tp = lax.axis_index("tp")
    group = place % groups
    patch = place // groups
    items_at = [(patch + o) % PATCHES for o in range(PATCHES)]
    scalars = jnp.stack([v.astype(jnp.int32) for v in items_at + [group, patch, tp]])
    both = ("req", "tp")

    columns = [[g + groups * p for p in range(PATCHES)] for g in range(groups)]
    rings = [[place * tps + t for place in column for t in range(tps)] for column in columns]

    def along_x(value, by):
        return lax.ppermute(value, "req", [(i, (i + by * groups) % slots) for i in range(slots)])

    raws = [lax.dynamic_index_in_dim(stale_kv[0], items_at[o], 1, keepdims=False) for o in range(1, PATCHES)]
    raws, scalars, w_own = lax.optimization_barrier((raws, scalars, w_out))
    kvs = [along_x(raws[o - 1], o) for o in range(1, PATCHES)]
    w_far = lax.ppermute(w_own, both, w_pairs)
    w_near = lax.ppermute(w_own, both, core_pairs)
    mod = jnp.transpose(modulation, (0, 2, 1, 3))
    q, k, v = project(scalars, hidden[0], mod, qk_gain, jnp.transpose(w_qkv, (1, 0, 2)), text_kv[0])
    q_sent, kvs = lax.optimization_barrier((q, kvs))
    q_all = lax.all_to_all(q_sent, "req", 0, 0, axis_index_groups=columns, tiled=True)
    w_across = lax.ppermute(w_far, both, core_pairs)
    owns = own_attention(scalars, q, k, v)
    near = [owns[0]] + [
        lax.ppermute(owns[g], "tp", [(i, i ^ g) for i in range(tps)]) for g in range(1, tps)
    ]
    sent = remote_attention(scalars, jnp.transpose(text_len), q_all, stale_kv[0], kvs)
    sent, near = lax.optimization_barrier((sent, near))
    far = lax.all_to_all(sent, both, 0, 0, axis_index_groups=rings, tiled=True)
    far = far.reshape(PATCHES, tps, *far.shape[1:])
    fresh = jnp.transpose(jnp.stack([k, v], axis=0), (2, 1, 0, 3))
    updated = finish(scalars, far, near, hidden[0], mod, [w_out, w_near, w_far, w_across])
    return (updated[None], fresh[None])


def solution(mesh):
    slots, tps = mesh.shape["req"], mesh.shape["tp"]
    groups = slots // PATCHES
    ring = 8
    w_pairs = []
    for place in range(slots):
        column, high = place // (ring // 2), place % (ring // 2)
        for t in range(tps):
            low, core = t // 2, t % 2
            z = 2 * high + low
            z = (z + (1 if low else -1)) % ring if core else z ^ 1
            target = column * (ring // 2) + z // 2
            w_pairs.append((place * tps + t, target * tps + z % 2 * 2 + core))
    core_pairs = [(i, i ^ 1) for i in range(slots * tps)]
    layout = (slots, tps, groups, w_pairs, core_pairs)
    return jax.shard_map(
        functools.partial(body, layout),
        mesh=mesh,
        in_specs=(
            P("req", None, None, None),
            P(),
            P(None, None, "tp"),
            P("tp", None),
            P(),
            P("req", None, None, None, "tp"),
            P("req", None, None, None, "tp"),
            P(),
        ),
        out_specs=(P("req", "tp", None, None), P("req", None, None, None, "tp")),
        check_vma=False,
    )
```
